32 devices in a mesh: rep: 16 (over z, y, core), fsdp: 2 (over x).
Axes of the slice: x: 2, y: 2, z: 4, core: 2. Of those that a mesh axis runs over, the one named last changes fastest.
Arguments:
- activations: bfloat16 [4096, 8192], P(('rep', 'fsdp')), may hold values from -7.75 to 7.75
- upstream: bfloat16 [4096, 512], P(('rep', 'fsdp')), may hold values from -0.484375 to 0.484375
- q_start: float32 [2, 4, 512], P('fsdp'), may hold values from -6 to 6
Outputs:
- error_feedback: bfloat16 [16, 8192, 512], P('rep', 'fsdp')
- p_basis: float32 [2, 4, 4096], P('fsdp')
- q_factor: float32 [2, 4, 512], P('fsdp')
The draws below stay inside these ranges and needn't reach their ends.
All inputs are finite; a program needn't handle non-finite values.
Results may differ from the reference program's by a relative error of at most 0.015.
Values may be sent and summed in bfloat16 or wider, within the bound.
A program may use at most 64 MiB of HBM per device.

```python
import jax
import jax.numpy as jnp
from jax import lax

D = 8192
KVW = 512
RANK = 4
TOK_DEV = 128
GROUP_TOKENS = 256
TOKENS = 4096
N_REP = 16
N_FSDP = 2


def unit_values(key, shape):
    return jnp.clip(jax.random.normal(key, shape, jnp.float32), -3.0, 3.0)


def noise_values(key, shape):
    return jnp.clip(jax.random.normal(key, shape, jnp.float32), -4.0, 4.0)


def shared_parts(key):
    strength = jnp.array([1.2, 1.0, 0.8, 0.6, 0.4], jnp.float32)
    tok_scale = GROUP_TOKENS ** (-0.25)
    weights = jnp.sqrt(strength) * tok_scale
    token_signs = jax.random.rademacher(jax.random.fold_in(key, 101), (TOKENS, 5), dtype=jnp.float32)
    left_dirs = unit_values(jax.random.fold_in(key, 102), (5, D))
    right_dirs = unit_values(jax.random.fold_in(key, 103), (5, KVW))
    return (token_signs * weights[None, :], left_dirs, right_dirs)


def draw_activations(key, part):
    coeffs, left_dirs, right_dirs = shared_parts(key)
    noise_part = noise_values(jax.random.fold_in(key, 104), (TOKENS, D))
    common = jnp.dot(coeffs, left_dirs, precision=lax.Precision.HIGHEST)
    return (noise_part + common).astype(jnp.bfloat16)


def draw_upstream(key, part):
    coeffs, left_dirs, right_dirs = shared_parts(key)
    noise_part = noise_values(jax.random.fold_in(key, 105), (TOKENS, KVW))
    common = jnp.dot(coeffs, right_dirs, precision=lax.Precision.HIGHEST)
    return ((noise_part + common) * GROUP_TOKENS ** (-0.5)).astype(jnp.bfloat16)


def block_levels(key, extent, cuts, least, high):
    def one(axis_at, shards_of):
        draws = jax.random.uniform(jax.random.fold_in(jax.random.fold_in(key, 6), axis_at), (shards_of,), jnp.float32, least / len(cuts), high / len(cuts))
        return jnp.repeat(jnp.exp(draws), extent[axis_at] // shards_of).reshape((-1,) + (1,) * (len(extent) - axis_at - 1))

    gain = one(*cuts[0])
    for cut in cuts[1:]:
        gain = gain * one(*cut)
    return gain


def noise(own_key, shape, deviation, limit, cuts=(), kind=jnp.bfloat16):
    values = deviation * jax.random.normal(own_key, shape, jnp.float32)
    if cuts:
        values = values * block_levels(own_key, shape, cuts, -0.22, 0.18)
    return jnp.clip(values, -limit, limit).astype(kind)


def setup_inputs(seed: int = 0) -> dict:
    streams_of = jax.random.split(jax.random.key(seed), 4)
    return {
        "activations": draw_activations(jax.random.fold_in(streams_of[3], 71), 0),
        "upstream": draw_upstream(jax.random.fold_in(streams_of[3], 71), 0),
        "q_start": noise(streams_of[2], (N_FSDP, RANK, KVW), 1.0, 6.0, ((0, 2),), jnp.float32),
    }


def replica_grad(xs, us):
    total = jnp.zeros((D, KVW), jnp.float32)
    for fidx in range(N_FSDP):
        part = jnp.dot(xs[fidx].T, us[fidx], preferred_element_type=jnp.float32).astype(jnp.bfloat16)
        part = lax.optimization_barrier(part)
        total = total + part.astype(jnp.float32)
    return total.reshape(N_FSDP, D // N_FSDP, KVW)

def orthonormal(rows_in):
    basis = []
    for i in range(RANK):
        vec = rows_in[i]
        for prev in basis:
            vec = vec - jnp.sum(vec * prev) * prev
        basis.append(vec / jnp.sqrt(jnp.sum(vec * vec) + 1e-06))
    return jnp.stack(basis)

def reference(activations, upstream, q_start):
    acts = activations.reshape(N_REP, N_FSDP, TOK_DEV, D)
    cots = upstream.reshape(N_REP, N_FSDP, TOK_DEV, KVW)
    high = lax.Precision.HIGHEST

    def left_step(carry, pair):
        mats = replica_grad(pair[0], pair[1])
        return (carry + jnp.einsum('frk,fnk->frn', q_start, mats, precision=high), None)
    p_sum, _ = lax.scan(left_step, jnp.zeros((N_FSDP, RANK, D // N_FSDP), jnp.float32), (acts, cots))
    p_basis = jax.vmap(orthonormal)(p_sum)

    def right_step(carry, pair):
        mats = replica_grad(pair[0], pair[1])
        return (carry + jnp.einsum('frn,fnk->frk', p_basis, mats, precision=high), None)
    q_factor, _ = lax.scan(right_step, jnp.zeros((N_FSDP, RANK, KVW), jnp.float32), (acts, cots))
    approx = jnp.einsum('frn,frk->fnk', p_basis, q_factor / N_REP, precision=high)

    def residual(pair):
        mats = replica_grad(pair[0], pair[1])
        return (mats - approx).astype(jnp.bfloat16).reshape(D, KVW)
    error_feedback = lax.map(residual, (acts, cots))
    return (error_feedback, p_basis, q_factor)
```

```python
import functools
import math

import jax
import jax.numpy as jnp
from jax import lax
from jax.experimental import pallas as pl
from jax.experimental.pallas import tpu as pltpu
from jax.sharding import PartitionSpec as P

MESH = pl.DeviceIdType.MESH
BF16 = jnp.bfloat16
F32 = jnp.float32


def two_terms(x):
    high = x.astype(BF16).astype(F32)
    return jnp.concatenate([high, x - high], axis=0).astype(BF16)


def folded(y):
    half = y.shape[0] // 2
    return y[:half] + y[half:]


def dot(a, b):
    return lax.dot_general(a, b, (((1,), (0,)), ((), ())), preferred_element_type=F32)


def dot_nt(a, b):
    return lax.dot_general(a, b, (((1,), (1,)), ((), ())), preferred_element_type=F32)


def exchange_kernel(
    cfg, act_hbm, up, q0, left_all, up_all, p_out, q_out,
    act, left, q_in, pc, pc_in, ps, rs_in, pfull, p_in, cc, c_in, g_in,
    local_sem, q_s, q_r, u_s, u_r, pc_s, pc_r, b_s, b_r, rs_s, rs_r, ag_s, ag_r,
    p_s, p_r, c_s, c_r, g_s, g_r,
):
    reps, groups, chunks, part1, part2, parts = cfg
    me = lax.axis_index("rep")
    mf = lax.axis_index("fsdp")
    tok, width = act.shape
    rows = width // groups
    stride = reps // chunks
    piece = rows // parts
    rank = q0.shape[1]
    cw = rows // chunks

    barrier = pltpu.get_barrier_semaphore()
    load = pltpu.make_async_copy(act_hbm, act, local_sem.at[0])
    load.start()

    def greet(d, _):
        pl.semaphore_signal(barrier, inc=1, device_id={"rep": lax.rem(me + d, reps)}, device_id_type=MESH)
        return 0

    for d in range(1, groups):
        pl.semaphore_signal(barrier, inc=1, device_id={"fsdp": lax.rem(mf + d, groups)}, device_id_type=MESH)
    lax.fori_loop(1, reps, greet, 0)
    keep_up = pltpu.make_async_copy(up, up_all.at[pl.ds(pl.multiple_of(mf * tok, tok), tok)], local_sem.at[1])
    keep_up.start()

    def to_group(d, src, dst, s, r):
        return pltpu.make_async_remote_copy(
            src_ref=src, dst_ref=dst, send_sem=s, recv_sem=r,
            device_id={"fsdp": lax.rem(mf + d, groups)}, device_id_type=MESH,
        )

    def to_rep(j, src, dst, s, r):
        return pltpu.make_async_remote_copy(
            src_ref=src, dst_ref=dst, send_sem=s, recv_sem=r,
            device_id={"rep": j}, device_id_type=MESH,
        )

    qs, us, bulk, pcs, pss, cs = [], [], [], [], [], []
    pl.semaphore_wait(barrier, reps - 1 + groups - 1)
    for d in range(1, groups):
        c = to_group(d, q0.at[0], q_in.at[d - 1], q_s.at[d - 1], q_r.at[d - 1])
        c.start()
        qs.append(c)
    for d in range(1, groups):
        c = to_group(
            d, up, up_all.at[pl.ds(pl.multiple_of(mf * tok, tok), tok)], u_s.at[d - 1], u_r.at[d - 1]
        )
        c.start()
        us.append(c)

    upv = up[...]
    load.wait()

    def columns(g):
        return pl.ds(pl.multiple_of(g * rows, rows), rows)

    def turn(i, _):
        at = pl.ds(pl.multiple_of(i * piece, piece), piece)
        left[at, :] = act[:, at].T
        return 0

    def project(qv, g):
        w = folded(dot_nt(two_terms(qv), upv))
        return folded(dot(two_terms(w), act[:, columns(g)]))

    for d in range(1, groups):
        qs[groups - d - 1].wait_recv()
        val = project(q_in[groups - d - 1], lax.rem(mf + d, groups))
        for c in range(chunks):
            pc[d - 1, c] = val[:, c * cw:(c + 1) * cw]
        cp = to_group(d, pc.at[d - 1], pc_in.at[d - 1], pc_s.at[d - 1], pc_r.at[d - 1])
        cp.start()
        pcs.append(cp)
    lax.fori_loop(0, groups * parts, turn, 0)

    for d in range(1, groups):
        g = lax.rem(mf + d, groups)
        row = []
        for k in range(parts):
            row.append(
                to_group(
                    d,
                    left.at[pl.ds(pl.multiple_of(g * rows + k * piece, piece), piece)],
                    left_all.at[pl.ds(k * piece, piece), pl.ds(pl.multiple_of(mf * tok, tok), tok)],
                    b_s.at[d - 1, k],
                    b_r.at[d - 1, k],
                )
            )
        bulk.append(row)

    def send_bulk(a, b):
        for k in range(a, b):
            for row in bulk:
                row[k].start()

    send_bulk(0, part1)
    keep_left = pltpu.make_async_copy(
        left.at[columns(mf)], left_all.at[:, pl.ds(pl.multiple_of(mf * tok, tok), tok)], local_sem.at[2]
    )
    keep_left.start()

    own = project(q0[0], mf)
    for c in range(chunks):
        ps[c] = own[:, c * cw:(c + 1) * cw]
    total = ps[...]
    for d in range(1, groups):
        pcs[d - 1].wait_recv()
        total = total + pc_in[d - 1]
    ps[...] = total

    mine = me // stride
    owner = lax.rem(me, stride) == 0

    def rs_copy(c):
        return to_rep(c * stride, ps.at[c], rs_in.at[me], rs_s.at[c], rs_r.at[me])

    def rs_from(j):
        return to_rep(j, rs_in.at[j], rs_in.at[j], rs_s.at[0], rs_r.at[j])

    def rs_send(d, _):
        c = lax.rem(mine + d, chunks)
        rs_copy(c).start()
        return 0

    def rs_done(d, _):
        c = lax.rem(mine + d, chunks)
        rs_copy(c).wait_send()
        return 0

    def ag_copy(j):
        return to_rep(j, pfull.at[mine], pfull.at[mine], ag_s.at[j], ag_r.at[mine])

    def ag_from(c):
        return to_rep(c * stride, pfull.at[c], pfull.at[c], ag_s.at[0], ag_r.at[c])

    lax.fori_loop(1, chunks, rs_send, 0)
    if stride > 1:
        @pl.when(jnp.logical_not(owner))
        def _():
            rs_copy(mine).start()

    def reduce_mine():
        rs_in[me] = ps[mine]

        def arrive(d, _):
            rs_from(lax.rem(me + d, reps)).wait_recv()
            return 0

        lax.fori_loop(1, reps, arrive, 0)
        pfull[mine] = jnp.sum(rs_in[...], axis=0)

        def share(d, _):
            ag_copy(lax.rem(me + d, reps)).start()
            return 0

        lax.fori_loop(1, reps, share, 0)

    def gather(d, _):
        ag_from(lax.rem(mine + d, chunks)).wait_recv()
        return 0

    if stride > 1:
        pl.when(owner)(reduce_mine)

        @pl.when(jnp.logical_not(owner))
        def _():
            ag_from(mine).wait_recv()
    else:
        reduce_mine()
    lax.fori_loop(1, chunks, gather, 0)

    v = pfull[...]
    row_at = lax.broadcasted_iota(jnp.int32, v.shape, 1)
    for i in range(rank):
        lead = v[:, i:i + 1, :]
        dots = jnp.sum(jnp.sum(v * lead, axis=0, keepdims=True), axis=2, keepdims=True)
        inv = lax.rsqrt(dots[:, i:i + 1, :] + 1e-06)
        unit = lead * inv
        v = jnp.where(row_at > i, v - (dots * inv) * unit, jnp.where(row_at == i, unit, v))
    for c in range(chunks):
        p_out[:, c * cw:(c + 1) * cw] = v[c]
    for d in range(1, groups):
        cp = to_group(d, p_out, p_in.at[d - 1], p_s.at[d - 1], p_r.at[d - 1])
        cp.start()
        pss.append(cp)
    send_bulk(part1, part2)

    def back(pv, g):
        t = folded(dot(two_terms(pv), left[columns(g), :]))
        return folded(dot(two_terms(t), upv))

    c_own = back(p_out[...], mf)
    for d in range(1, groups):
        pss[groups - d - 1].wait_recv()
        cc[d - 1] = back(p_in[groups - d - 1], lax.rem(mf + d, groups))
        cp = to_group(d, cc.at[d - 1], c_in.at[d - 1], c_s.at[d - 1], c_r.at[d - 1])
        cp.start()
        cs.append(cp)
    send_bulk(part2, parts)
    for d in range(1, groups):
        cs[d - 1].wait_recv()
        c_own = c_own + c_in[d - 1]
    g_in[me] = c_own

    def g_copy(j):
        return to_rep(j, g_in.at[me], g_in.at[me], g_s.at[j], g_r.at[me])

    def g_send(d, _):
        g_copy(lax.rem(me + d, reps)).start()
        return 0

    def g_arrive(d, _):
        j = lax.rem(me + d, reps)
        to_rep(j, g_in.at[j], g_in.at[j], g_s.at[0], g_r.at[j]).wait_recv()
        return 0

    def g_done(d, _):
        g_copy(lax.rem(me + d, reps)).wait_send()
        return 0

    def ag_done(d, _):
        ag_copy(lax.rem(me + d, reps)).wait_send()
        return 0

    lax.fori_loop(1, reps, g_send, 0)
    lax.fori_loop(1, reps, g_arrive, 0)
    q_out[...] = jnp.sum(g_in[...], axis=0)

    lax.fori_loop(1, chunks, rs_done, 0)
    if stride > 1:
        @pl.when(jnp.logical_not(owner))
        def _():
            rs_copy(mine).wait_send()

        @pl.when(owner)
        def _():
            lax.fori_loop(1, reps, ag_done, 0)
    else:
        lax.fori_loop(1, reps, ag_done, 0)
    lax.fori_loop(1, reps, g_done, 0)
    for c in qs + pcs + pss + cs:
        c.wait_send()
    keep_up.wait()
    keep_left.wait()
    for c in us:
        c.wait()
    for k in range(parts):
        for row in bulk:
            row[k].wait()


def residual_kernel(reps, left, up, p, q, err, p_out, q_out):
    pv, qv = p[...], q[...]
    q_out[0] = qv
    p_out[0] = pv
    scaled = qv * (-1.0 / reps) if reps & (reps - 1) == 0 else -(qv / reps)
    ph = pv.astype(BF16).astype(F32)
    qh = scaled.astype(BF16).astype(F32)
    pst = jnp.concatenate([ph, pv - ph, ph, pv - ph], axis=0).astype(BF16)
    qst = jnp.concatenate([qh, qh, scaled - qh, scaled - qh], axis=0).astype(BF16)
    low = lax.dot_general(pst, qst, (((0,), (0,)), ((), ())), preferred_element_type=F32)
    err[0] = (dot(left[...], up[...]) + low).astype(BF16)


def on_device(activations, upstream, q_start):
    reps = lax.axis_size("rep")
    groups = lax.axis_size("fsdp")
    tok, width = activations.shape
    kvw = upstream.shape[1]
    rank = q_start.shape[1]
    rows = width // groups
    chunks = math.gcd(reps, rows // 128)
    cw = rows // chunks
    parts = 8
    cfg = (reps, groups, chunks, 3, 5, parts)
    vm = pl.BlockSpec(memory_space=pltpu.VMEM)
    hbm = pl.BlockSpec(memory_space=pl.ANY)
    dma = pltpu.SemaphoreType.DMA
    peers = groups - 1
    left_all, up_all, p_basis, q_factor = pl.pallas_call(
        functools.partial(exchange_kernel, cfg),
        out_shape=(
            jax.ShapeDtypeStruct((rows, groups * tok), BF16),
            jax.ShapeDtypeStruct((groups * tok, kvw), BF16),
            jax.ShapeDtypeStruct((rank, rows), F32),
            jax.ShapeDtypeStruct((rank, kvw), F32),
        ),
        in_specs=[hbm, vm, vm],
        out_specs=(hbm, hbm, vm, vm),
        scratch_shapes=[
            pltpu.VMEM((tok, width), BF16),
            pltpu.VMEM((width, tok), BF16),
            pltpu.VMEM((peers, rank, kvw), F32),
            pltpu.VMEM((peers, chunks, rank, cw), F32),
            pltpu.VMEM((peers, chunks, rank, cw), F32),
            pltpu.VMEM((chunks, rank, cw), F32),
            pltpu.VMEM((reps, rank, cw), F32),
            pltpu.VMEM((chunks, rank, cw), F32),
            pltpu.VMEM((peers, rank, rows), F32),
            pltpu.VMEM((peers, rank, kvw), F32),
            pltpu.VMEM((peers, rank, kvw), F32),
            pltpu.VMEM((reps, rank, kvw), F32),
            dma((3,)),
            dma((peers,)), dma((peers,)),
            dma((peers,)), dma((peers,)),
            dma((peers,)), dma((peers,)),
            dma((peers, parts)), dma((peers, parts)),
            dma((chunks,)), dma((reps,)),
            dma((reps,)), dma((chunks,)),
            dma((peers,)), dma((peers,)),
            dma((peers,)), dma((peers,)),
            dma((reps,)), dma((reps,)),
        ],
        compiler_params=pltpu.CompilerParams(collective_id=0, has_side_effects=True),
        name="exchange",
    )(activations, upstream, q_start)
    step = rows // 8
    return pl.pallas_call(
        functools.partial(residual_kernel, reps),
        grid=(8,),
        out_shape=(
            jax.ShapeDtypeStruct((1, rows, kvw), BF16),
            jax.ShapeDtypeStruct((1, rank, rows), F32),
            jax.ShapeDtypeStruct((1, rank, kvw), F32),
        ),
        in_specs=[
            pl.BlockSpec((step, groups * tok), lambda i: (i, 0)),
            pl.BlockSpec((groups * tok, kvw), lambda i: (0, 0)),
            pl.BlockSpec((rank, step), lambda i: (0, i)),
            pl.BlockSpec((rank, kvw), lambda i: (0, 0)),
        ],
        out_specs=(
            pl.BlockSpec((1, step, kvw), lambda i: (0, i, 0)),
            pl.BlockSpec((1, rank, step), lambda i: (0, 0, i)),
            pl.BlockSpec((1, rank, kvw), lambda i: (0, 0, 0)),
        ),
        name="residual",
    )(left_all, up_all, p_basis, q_factor)


def solution(mesh):
    in_specs = (P(("rep", "fsdp"), None), P(("rep", "fsdp"), None), P("fsdp", None, None))
    out_specs = (P("rep", "fsdp", None), P("fsdp", None, None), P("fsdp", None, None))
    return jax.shard_map(
        on_device, mesh=mesh, in_specs=in_specs, out_specs=out_specs, check_vma=False
    )
```

```python
import functools
import math

import jax
import jax.numpy as jnp
from jax import lax
from jax.experimental import pallas as pl
from jax.experimental.pallas import tpu as pltpu
from jax.sharding import PartitionSpec as P

MESH = pl.DeviceIdType.MESH
BF16 = jnp.bfloat16
F32 = jnp.float32


def two_terms(x):
    high = x.astype(BF16).astype(F32)
    return jnp.concatenate([high, x - high], axis=0).astype(BF16)


def folded(y):
    half = y.shape[0] // 2
    return y[:half] + y[half:]


def dot(a, b):
    return lax.dot_general(a, b, (((1,), (0,)), ((), ())), preferred_element_type=F32)


def dot_nt(a, b):
    return lax.dot_general(a, b, (((1,), (1,)), ((), ())), preferred_element_type=F32)


def exchange_kernel(
    cfg, act_hbm, up, q0, left_all, up_all, p_out, q_out,
    act, left, q_in, pc, rs_in, pfull, p_flat, cc, c_in, g_in,
    local_sem, q_s, q_r, u_s, u_r, b_s, b_r, rs_s, rs_r, ag_s, ag_r, c_s, c_r, g_s, g_r,
):
    reps, groups, chunks, part1, part2, parts = cfg
    me = lax.axis_index("rep")
    mf = lax.axis_index("fsdp")
    tok, width = act.shape
    rows = width // groups
    stride = reps // chunks
    piece = rows // parts
    rank = q0.shape[1]
    cw = rows // chunks

    def ahead(d):
        return lax.rem(mf + d, groups)

    def remote(rep, group, src, dst, s, r):
        return pltpu.make_async_remote_copy(
            src_ref=src, dst_ref=dst, send_sem=s, recv_sem=r,
            device_id={"rep": rep, "fsdp": group}, device_id_type=MESH,
        )

    def loop(a, b, fn):
        def body(i, carry):
            fn(i)
            return carry

        lax.fori_loop(a, b, body, 0)

    load = pltpu.make_async_copy(act_hbm, act, local_sem.at[0])
    load.start()
    barrier = pltpu.get_barrier_semaphore()
    for f in range(groups):
        def greet(d):
            pl.semaphore_signal(
                barrier, inc=1, device_id={"rep": lax.rem(me + d, reps), "fsdp": ahead(f)},
                device_id_type=MESH,
            )

        loop(0 if f else 1, reps, greet)
    my_tokens = pl.ds(pl.multiple_of(mf * tok, tok), tok)
    keep_up = pltpu.make_async_copy(up, up_all.at[my_tokens], local_sem.at[1])
    keep_up.start()
    upv = up[...]

    def columns(g):
        return pl.ds(pl.multiple_of(g * rows, rows), rows)

    def project(qv, g):
        w = folded(dot_nt(two_terms(qv), upv))
        val = folded(dot(two_terms(w), act[:, columns(g)]))
        for c in range(chunks):
            pc[g, c] = val[:, c * cw:(c + 1) * cw]

    def turn(i):
        at = pl.ds(pl.multiple_of(i * piece, piece), piece)
        left[at, :] = act[:, at].T

    load.wait()
    project(q0[0], mf)
    loop(0, groups * parts, turn)
    keep_left = pltpu.make_async_copy(left.at[columns(mf)], left_all.at[:, my_tokens], local_sem.at[2])
    keep_left.start()
    pl.semaphore_wait(barrier, reps * groups - 1)

    qs, us, bulk, cs = [], [], [], []
    for d in range(1, groups):
        qs.append(remote(me, ahead(d), q0.at[0], q_in.at[d - 1], q_s.at[d - 1], q_r.at[d - 1]))
        qs[-1].start()
    for d in range(1, groups):
        us.append(remote(me, ahead(d), up, up_all.at[my_tokens], u_s.at[d - 1], u_r.at[d - 1]))
        us[-1].start()

    mine = me // stride
    owner = lax.rem(me, stride) == 0
    my_slot = mf * reps + me

    def rs_copy(g, c):
        return remote(c * stride, g, pc.at[g, c], rs_in.at[my_slot], rs_s.at[g, c], rs_r.at[my_slot])

    def rs_all(g, act_on, own_shard):
        if own_shard:
            loop(1, chunks, lambda d: act_on(rs_copy(g, lax.rem(mine + d, chunks))))
            if stride > 1:
                @pl.when(jnp.logical_not(owner))
                def _():
                    act_on(rs_copy(g, mine))
        else:
            loop(0, chunks, lambda d: act_on(rs_copy(g, lax.rem(mine + d, chunks))))

    rs_all(mf, lambda c: c.start(), True)
    for d in range(1, groups):
        qs[groups - d - 1].wait_recv()
        project(q_in[groups - d - 1], ahead(d))
        rs_all(ahead(d), lambda c: c.start(), False)

    for d in range(1, groups):
        bulk.append([
            remote(
                me, ahead(d),
                left.at[pl.ds(pl.multiple_of(ahead(d) * rows + k * piece, piece), piece)],
                left_all.at[pl.ds(k * piece, piece), my_tokens],
                b_s.at[d - 1, k], b_r.at[d - 1, k],
            )
            for k in range(parts)
        ])

    def send_bulk(a, b):
        for k in range(a, b):
            for row in bulk:
                row[k].start()

    send_bulk(0, part1)

    def ag_copy(rep, g):
        return remote(
            rep, g, pfull.at[mf, mine], pfull.at[mf, mine], ag_s.at[g * reps + rep], ag_r.at[mf * chunks + mine]
        )

    def ag_all(act_on):
        for d in list(range(1, groups)) + [0]:
            loop(0 if d else 1, reps, lambda i: act_on(ag_copy(lax.rem(me + i, reps), ahead(d))))

    def reduce_mine():
        rs_in[my_slot] = pc[mf, mine]

        def arrive(i):
            j = lax.rem(my_slot + i, reps * groups)
            remote(
                lax.rem(j, reps), j // reps, rs_in.at[j], rs_in.at[j], rs_s.at[0, 0], rs_r.at[j]
            ).wait_recv()

        loop(1, reps * groups, arrive)
        pfull[mf, mine] = jnp.sum(rs_in[...], axis=0)
        ag_all(lambda c: c.start())

    def gather(i):
        j = lax.rem(mf * chunks + mine + i, groups * chunks)
        g, c = j // chunks, lax.rem(j, chunks)
        remote(c * stride, g, pfull.at[g, c], pfull.at[g, c], ag_s.at[0], ag_r.at[j]).wait_recv()

    if stride > 1:
        pl.when(owner)(reduce_mine)
        pl.when(jnp.logical_not(owner))(lambda: gather(0))
    else:
        reduce_mine()
    send_bulk(part1, part2)
    loop(1, groups * chunks, gather)

    v = pfull[...]
    row_at = lax.broadcasted_iota(jnp.int32, v.shape, 2)
    for i in range(rank):
        lead = v[:, :, i:i + 1, :]
        dots = jnp.sum(jnp.sum(v * lead, axis=1, keepdims=True), axis=3, keepdims=True)
        inv = lax.rsqrt(dots[:, :, i:i + 1, :] + 1e-06)
        unit = lead * inv
        v = jnp.where(row_at > i, v - (dots * inv) * unit, jnp.where(row_at == i, unit, v))
    for g in range(groups):
        for c in range(chunks):
            p_flat[g, :, c * cw:(c + 1) * cw] = v[g, c]
        t = folded(dot(two_terms(p_flat[g]), left[g * rows:(g + 1) * rows, :]))
        cc[g] = folded(dot(two_terms(t), upv))
    for d in range(1, groups):
        g = ahead(d)
        cs.append(remote(me, g, cc.at[g], c_in.at[d - 1], c_s.at[d - 1], c_r.at[d - 1]))
        cs[-1].start()
    send_bulk(part2, parts)
    p_out[...] = p_flat[mf]
    total = cc[mf]
    for c, got in zip(cs, range(groups - 1)):
        c.wait_recv()
        total = total + c_in[got]
    g_in[me] = total

    def g_copy(i):
        j = lax.rem(me + i, reps)
        return remote(j, mf, g_in.at[me], g_in.at[me], g_s.at[j], g_r.at[me])

    def g_arrive(i):
        j = lax.rem(me + i, reps)
        remote(j, mf, g_in.at[j], g_in.at[j], g_s.at[0], g_r.at[j]).wait_recv()

    loop(1, reps, lambda i: g_copy(i).start())
    loop(1, reps, g_arrive)
    q_out[...] = jnp.sum(g_in[...], axis=0)

    for c in qs + cs:
        c.wait_send()
    for d in range(groups):
        rs_all(ahead(d), lambda c: c.wait_send(), d == 0)
    if stride > 1:
        pl.when(owner)(lambda: ag_all(lambda c: c.wait_send()))
    else:
        ag_all(lambda c: c.wait_send())
    loop(1, reps, lambda i: g_copy(i).wait_send())
    keep_up.wait()
    keep_left.wait()
    for c in us:
        c.wait()
    for k in range(parts):
        for row in bulk:
            row[k].wait()


def residual_kernel(
    reps, left_hbm, up_hbm, p_hbm, q_hbm, err, p_out, q_out, left, up, p, q, out, in_sem, left_sem, out_sem
):
    parts, step = left.shape[0], left.shape[1]
    small = [
        pltpu.make_async_copy(src, dst, in_sem.at[i])
        for i, (src, dst) in enumerate(((q_hbm, q), (p_hbm, p), (up_hbm, up)))
    ]
    loads = [
        pltpu.make_async_copy(left_hbm.at[pl.ds(k * step, step)], left.at[k], left_sem.at[k])
        for k in range(parts)
    ]
    for c in small + loads:
        c.start()
    for c in small:
        c.wait()
    stores = [
        pltpu.make_async_copy(p, p_out.at[0], out_sem.at[parts]),
        pltpu.make_async_copy(q, q_out.at[0], out_sem.at[parts + 1]),
    ]
    for c in stores:
        c.start()
    upv = up[...]
    scaled = -(q[...] / reps)
    qh = scaled.astype(BF16).astype(F32)
    qst = jnp.concatenate([qh, qh, scaled - qh, scaled - qh], axis=0).astype(BF16)
    for k in range(parts):
        pv = p[:, k * step:(k + 1) * step]
        ph = pv.astype(BF16).astype(F32)
        pst = jnp.concatenate([ph, pv - ph, ph, pv - ph], axis=0).astype(BF16)
        low = lax.dot_general(pst, qst, (((0,), (0,)), ((), ())), preferred_element_type=F32)
        loads[k].wait()
        out[k] = (dot(left[k], upv) + low).astype(BF16)
        c = pltpu.make_async_copy(out.at[k], err.at[0, pl.ds(k * step, step)], out_sem.at[k])
        c.start()
        stores.append(c)
    for c in stores:
        c.wait()


def on_device(activations, upstream, q_start):
    reps = lax.axis_size("rep")
    groups = lax.axis_size("fsdp")
    tok, width = activations.shape
    kvw = upstream.shape[1]
    rank = q_start.shape[1]
    rows = width // groups
    chunks = math.gcd(reps, rows // 128)
    cw = rows // chunks
    parts = 16
    cfg = (reps, groups, chunks, 4, 9, parts)
    vm = pl.BlockSpec(memory_space=pltpu.VMEM)
    hbm = pl.BlockSpec(memory_space=pl.ANY)
    dma = pltpu.SemaphoreType.DMA
    peers = groups - 1
    left_all, up_all, p_basis, q_factor = pl.pallas_call(
        functools.partial(exchange_kernel, cfg),
        out_shape=(
            jax.ShapeDtypeStruct((rows, groups * tok), BF16),
            jax.ShapeDtypeStruct((groups * tok, kvw), BF16),
            jax.ShapeDtypeStruct((rank, rows), F32),
            jax.ShapeDtypeStruct((rank, kvw), F32),
        ),
        in_specs=[hbm, vm, vm],
        out_specs=(hbm, hbm, vm, vm),
        scratch_shapes=[
            pltpu.VMEM((tok, width), BF16),
            pltpu.VMEM((width, tok), BF16),
            pltpu.VMEM((peers, rank, kvw), F32),
            pltpu.VMEM((groups, chunks, rank, cw), F32),
            pltpu.VMEM((groups * reps, rank, cw), F32),
            pltpu.VMEM((groups, chunks, rank, cw), F32),
            pltpu.VMEM((groups, rank, rows), F32),
            pltpu.VMEM((groups, rank, kvw), F32),
            pltpu.VMEM((peers, rank, kvw), F32),
            pltpu.VMEM((reps, rank, kvw), F32),
            dma((3,)),
            dma((peers,)), dma((peers,)),
            dma((peers,)), dma((peers,)),
            dma((peers, parts)), dma((peers, parts)),
            dma((groups, chunks)), dma((groups * reps,)),
            dma((groups * reps,)), dma((groups * chunks,)),
            dma((peers,)), dma((peers,)),
            dma((reps,)), dma((reps,)),
        ],
        compiler_params=pltpu.CompilerParams(collective_id=0, has_side_effects=True),
        name="exchange",
    )(activations, upstream, q_start)
    steps = 8
    step = rows // steps
    return pl.pallas_call(
        functools.partial(residual_kernel, reps),
        out_shape=(
            jax.ShapeDtypeStruct((1, rows, kvw), BF16),
            jax.ShapeDtypeStruct((1, rank, rows), F32),
            jax.ShapeDtypeStruct((1, rank, kvw), F32),
        ),
        in_specs=[hbm] * 4,
        out_specs=(hbm,) * 3,
        scratch_shapes=[
            pltpu.VMEM((steps, step, groups * tok), BF16),
            pltpu.VMEM((groups * tok, kvw), BF16),
            pltpu.VMEM((rank, rows), F32),
            pltpu.VMEM((rank, kvw), F32),
            pltpu.VMEM((steps, step, kvw), BF16),
            dma((3,)), dma((steps,)), dma((steps + 2,)),
        ],
        name="residual",
    )(left_all, up_all, p_basis, q_factor)


def solution(mesh):
    in_specs = (P(("rep", "fsdp"), None), P(("rep", "fsdp"), None), P("fsdp", None, None))
    out_specs = (P("rep", "fsdp", None), P("fsdp", None, None), P("fsdp", None, None))
    return jax.shard_map(
        on_device, mesh=mesh, in_specs=in_specs, out_specs=out_specs, check_vma=False
    )
```

```python
import functools
import math

import jax
import jax.numpy as jnp
from jax import lax
from jax.experimental import pallas as pl
from jax.experimental.pallas import tpu as pltpu
from jax.sharding import PartitionSpec as P

MESH = pl.DeviceIdType.MESH
BF16 = jnp.bfloat16
F32 = jnp.float32


def two_terms(x):
    high = x.astype(BF16).astype(F32)
    return jnp.concatenate([high, x - high], axis=0).astype(BF16)


def folded(y):
    half = y.shape[0] // 2
    return y[:half] + y[half:]


def dot(a, b):
    return lax.dot_general(a, b, (((1,), (0,)), ((), ())), preferred_element_type=F32)


def dot_nt(a, b):
    return lax.dot_general(a, b, (((1,), (1,)), ((), ())), preferred_element_type=F32)


def exchange_kernel(
    cfg, act_hbm, up, q0, left_all, up_all, p_out, g_in,
    act, up_v, q_v, left, q_in, pc, rs_in, pfull, p_flat, cc, c_in, g_own,
    local_sem, q_s, q_r, u_s, u_r, b_s, b_r, rs_s, rs_r, ag_s, ag_r, c_s, c_r, g_s, g_r,
):
    reps, groups, chunks, part1, part2, parts = cfg
    me = lax.axis_index("rep")
    mf = lax.axis_index("fsdp")
    tok, width = act.shape
    rows = width // groups
    stride = reps // chunks
    piece = rows // parts
    rank = q_v.shape[0]
    cw = rows // chunks

    def ahead(d):
        return lax.rem(mf + d, groups)

    def remote(rep, group, src, dst, s, r):
        return pltpu.make_async_remote_copy(
            src_ref=src, dst_ref=dst, send_sem=s, recv_sem=r,
            device_id={"rep": rep, "fsdp": group}, device_id_type=MESH,
        )

    def loop(a, b, fn):
        def body(i, carry):
            fn(i)
            return carry

        lax.fori_loop(a, b, body, 0)

    load = pltpu.make_async_copy(act_hbm, act, local_sem.at[0])
    load_q = pltpu.make_async_copy(q0.at[0], q_v, local_sem.at[3])
    load_up = pltpu.make_async_copy(up, up_v, local_sem.at[4])
    load_q.start()
    load_up.start()
    load.start()
    barrier = pltpu.get_barrier_semaphore()
    for f in range(groups):
        def greet(d):
            pl.semaphore_signal(
                barrier, inc=1, device_id={"rep": lax.rem(me + d, reps), "fsdp": ahead(f)},
                device_id_type=MESH,
            )

        loop(0 if f else 1, reps, greet)
    my_tokens = pl.ds(pl.multiple_of(mf * tok, tok), tok)
    load_q.wait()
    load_up.wait()
    keep_up = pltpu.make_async_copy(up_v, up_all.at[my_tokens], local_sem.at[1])
    keep_up.start()
    upv = up_v[...]

    def columns(g):
        return pl.ds(pl.multiple_of(g * rows, rows), rows)

    def project(qv, g):
        w = folded(dot_nt(two_terms(qv), upv))
        val = folded(dot(two_terms(w), act[:, columns(g)]))
        for c in range(chunks):
            pc[g, c] = val[:, c * cw:(c + 1) * cw]

    def turn(i):
        at = pl.ds(pl.multiple_of(i * piece, piece), piece)
        left[at, :] = act[:, at].T

    load.wait()
    loop(0, (groups - 1) * parts, lambda i: turn(lax.rem(mf * parts + parts + i, groups * parts)))
    project(q_v[...], mf)
    keep_left = pltpu.make_async_copy(left.at[columns(mf)], left_all.at[:, my_tokens], local_sem.at[2])
    pl.semaphore_wait(barrier, reps * groups - 1)

    qs, us, bulk, cs = [], [], [], []
    for d in range(1, groups):
        qs.append(remote(me, ahead(d), q0.at[0], q_in.at[d - 1], q_s.at[d - 1], q_r.at[d - 1]))
        qs[-1].start()
    for d in range(1, groups):
        us.append(remote(me, ahead(d), up, up_all.at[my_tokens], u_s.at[d - 1], u_r.at[d - 1]))
        us[-1].start()

    mine = me // stride
    owner = lax.rem(me, stride) == 0
    my_slot = mf * reps + me

    def rs_copy(g, c):
        return remote(c * stride, g, pc.at[g, c], rs_in.at[my_slot], rs_s.at[g, c], rs_r.at[my_slot])

    def rs_all(g, act_on, own_shard):
        if own_shard:
            loop(1, chunks, lambda d: act_on(rs_copy(g, lax.rem(mine + d, chunks))))
            if stride > 1:
                @pl.when(jnp.logical_not(owner))
                def _():
                    act_on(rs_copy(g, mine))
        else:
            loop(0, chunks, lambda d: act_on(rs_copy(g, lax.rem(mine + d, chunks))))

    rs_all(mf, lambda c: c.start(), True)
    loop(0, parts, lambda i: turn(mf * parts + i))
    keep_left.start()
    for d in range(1, groups):
        qs[groups - d - 1].wait_recv()
        project(q_in[groups - d - 1], ahead(d))
        rs_all(ahead(d), lambda c: c.start(), False)

    for d in range(1, groups):
        bulk.append([
            remote(
                me, ahead(d),
                left.at[pl.ds(pl.multiple_of(ahead(d) * rows + k * piece, piece), piece)],
                left_all.at[pl.ds(k * piece, piece), my_tokens],
                b_s.at[d - 1, k], b_r.at[d - 1, k],
            )
            for k in range(parts)
        ])

    def send_bulk(a, b):
        for k in range(a, b):
            for row in bulk:
                row[k].start()

    send_bulk(0, part1)

    def ag_copy(rep, g):
        return remote(
            rep, g, pfull.at[mf, mine], pfull.at[mf, mine], ag_s.at[g * reps + rep], ag_r.at[mf * chunks + mine]
        )

    def ag_all(act_on):
        for d in list(range(1, groups)) + [0]:
            loop(0 if d else 1, reps, lambda i: act_on(ag_copy(lax.rem(me + i, reps), ahead(d))))

    def reduce_mine():
        rs_in[my_slot] = pc[mf, mine]

        def arrive(i):
            j = lax.rem(my_slot + i, reps * groups)
            remote(
                lax.rem(j, reps), j // reps, rs_in.at[j], rs_in.at[j], rs_s.at[0, 0], rs_r.at[j]
            ).wait_recv()

        loop(1, reps * groups, arrive)
        pfull[mf, mine] = jnp.sum(rs_in[...], axis=0)
        ag_all(lambda c: c.start())

    def gather(i):
        j = lax.rem(mf * chunks + mine + i, groups * chunks)
        g, c = j // chunks, lax.rem(j, chunks)
        remote(c * stride, g, pfull.at[g, c], pfull.at[g, c], ag_s.at[0], ag_r.at[j]).wait_recv()

    if stride > 1:
        pl.when(owner)(reduce_mine)
        pl.when(jnp.logical_not(owner))(lambda: gather(0))
    else:
        reduce_mine()
    send_bulk(part1, part2)
    loop(1, groups * chunks, gather)

    v = pfull[...]
    row_at = lax.broadcasted_iota(jnp.int32, v.shape, 2)
    for i in range(rank):
        lead = v[:, :, i:i + 1, :]
        dots = jnp.sum(jnp.sum(v * lead, axis=1, keepdims=True), axis=3, keepdims=True)
        inv = lax.rsqrt(dots[:, :, i:i + 1, :] + 1e-06)
        unit = lead * inv
        v = jnp.where(row_at > i, v - (dots * inv) * unit, jnp.where(row_at == i, unit, v))
    for g in range(groups):
        for c in range(chunks):
            p_flat[g, :, c * cw:(c + 1) * cw] = v[g, c]
        t = folded(dot(two_terms(p_flat[g]), left[g * rows:(g + 1) * rows, :]))
        cc[g] = folded(dot(two_terms(t), upv))
    keep_p = pltpu.make_async_copy(p_flat.at[mf], p_out, local_sem.at[5])
    for d in range(1, groups):
        g = ahead(d)
        cs.append(remote(me, g, cc.at[g], c_in.at[d - 1], c_s.at[d - 1], c_r.at[d - 1]))
        cs[-1].start()
    send_bulk(part2, parts)
    keep_p.start()
    total = cc[mf]
    for c, got in zip(cs, range(groups - 1)):
        c.wait_recv()
        total = total + c_in[got]
    g_own[...] = total
    keep_g = pltpu.make_async_copy(g_own, g_in.at[me], local_sem.at[6])

    def g_copy(i):
        j = lax.rem(me + i, reps)
        return remote(j, mf, g_own, g_in.at[me], g_s.at[j], g_r.at[me])

    def g_arrive(i):
        j = lax.rem(me + i, reps)
        remote(j, mf, g_in.at[j], g_in.at[j], g_s.at[0], g_r.at[j]).wait_recv()

    loop(1, reps, lambda i: g_copy(i).start())
    keep_g.start()
    loop(1, reps, g_arrive)

    for c in qs + cs:
        c.wait_send()
    for d in range(groups):
        rs_all(ahead(d), lambda c: c.wait_send(), d == 0)
    if stride > 1:
        pl.when(owner)(lambda: ag_all(lambda c: c.wait_send()))
    else:
        ag_all(lambda c: c.wait_send())
    loop(1, reps, lambda i: g_copy(i).wait_send())
    keep_up.wait()
    keep_left.wait()
    keep_p.wait()
    keep_g.wait()
    for c in us:
        c.wait()
    for k in range(parts):
        for row in bulk:
            row[k].wait()


def residual_kernel(
    reps, left_hbm, up_hbm, p_hbm, g_hbm, err, p_out, q_out, left, up, p, g, q, out, in_sem, left_sem, out_sem
):
    parts, step = left.shape[0], left.shape[1]
    small = [
        pltpu.make_async_copy(src, dst, in_sem.at[i])
        for i, (src, dst) in enumerate(((g_hbm, g), (p_hbm, p), (up_hbm, up)))
    ]
    loads = [
        pltpu.make_async_copy(left_hbm.at[pl.ds(k * step, step)], left.at[k], left_sem.at[k])
        for k in range(parts)
    ]
    for c in small + loads:
        c.start()
    for c in small:
        c.wait()
    q[...] = jnp.sum(g[...], axis=0)
    stores = [
        pltpu.make_async_copy(p, p_out.at[0], out_sem.at[parts]),
        pltpu.make_async_copy(q, q_out.at[0], out_sem.at[parts + 1]),
    ]
    for c in stores:
        c.start()
    upv = up[...]
    scaled = -(q[...] / reps)
    qh = scaled.astype(BF16).astype(F32)
    qst = jnp.concatenate([qh, qh, scaled - qh, scaled - qh], axis=0).astype(BF16)
    for k in range(parts):
        pv = p[:, k * step:(k + 1) * step]
        ph = pv.astype(BF16).astype(F32)
        pst = jnp.concatenate([ph, pv - ph, ph, pv - ph], axis=0).astype(BF16)
        low = lax.dot_general(pst, qst, (((0,), (0,)), ((), ())), preferred_element_type=F32)
        loads[k].wait()
        out[k] = (dot(left[k], upv) + low).astype(BF16)
        c = pltpu.make_async_copy(out.at[k], err.at[0, pl.ds(k * step, step)], out_sem.at[k])
        c.start()
        stores.append(c)
    for c in stores:
        c.wait()


def on_device(activations, upstream, q_start):
    reps = lax.axis_size("rep")
    groups = lax.axis_size("fsdp")
    tok, width = activations.shape
    kvw = upstream.shape[1]
    rank = q_start.shape[1]
    rows = width // groups
    chunks = math.gcd(reps, rows // 128)
    cw = rows // chunks
    parts = 16
    cfg = (reps, groups, chunks, 5, 10, parts)
    hbm = pl.BlockSpec(memory_space=pl.ANY)
    dma = pltpu.SemaphoreType.DMA
    peers = groups - 1
    left_all, up_all, p_basis, q_terms = pl.pallas_call(
        functools.partial(exchange_kernel, cfg),
        out_shape=(
            jax.ShapeDtypeStruct((rows, groups * tok), BF16),
            jax.ShapeDtypeStruct((groups * tok, kvw), BF16),
            jax.ShapeDtypeStruct((rank, rows), F32),
            jax.ShapeDtypeStruct((reps, rank, kvw), F32),
        ),
        in_specs=[hbm] * 3,
        out_specs=(hbm,) * 4,
        scratch_shapes=[
            pltpu.VMEM((tok, width), BF16),
            pltpu.VMEM((tok, kvw), BF16),
            pltpu.VMEM((rank, kvw), F32),
            pltpu.VMEM((width, tok), BF16),
            pltpu.VMEM((peers, rank, kvw), F32),
            pltpu.VMEM((groups, chunks, rank, cw), F32),
            pltpu.VMEM((groups * reps, rank, cw), F32),
            pltpu.VMEM((groups, chunks, rank, cw), F32),
            pltpu.VMEM((groups, rank, rows), F32),
            pltpu.VMEM((groups, rank, kvw), F32),
            pltpu.VMEM((peers, rank, kvw), F32),
            pltpu.VMEM((rank, kvw), F32),
            dma((7,)),
            dma((peers,)), dma((peers,)),
            dma((peers,)), dma((peers,)),
            dma((peers, parts)), dma((peers, parts)),
            dma((groups, chunks)), dma((groups * reps,)),
            dma((groups * reps,)), dma((groups * chunks,)),
            dma((peers,)), dma((peers,)),
            dma((reps,)), dma((reps,)),
        ],
        compiler_params=pltpu.CompilerParams(collective_id=0, has_side_effects=True),
        name="exchange",
    )(activations, upstream, q_start)
    steps = 8
    step = rows // steps
    return pl.pallas_call(
        functools.partial(residual_kernel, reps),
        out_shape=(
            jax.ShapeDtypeStruct((1, rows, kvw), BF16),
            jax.ShapeDtypeStruct((1, rank, rows), F32),
            jax.ShapeDtypeStruct((1, rank, kvw), F32),
        ),
        in_specs=[hbm] * 4,
        out_specs=(hbm,) * 3,
        scratch_shapes=[
            pltpu.VMEM((steps, step, groups * tok), BF16),
            pltpu.VMEM((groups * tok, kvw), BF16),
            pltpu.VMEM((rank, rows), F32),
            pltpu.VMEM((reps, rank, kvw), F32),
            pltpu.VMEM((rank, kvw), F32),
            pltpu.VMEM((steps, step, kvw), BF16),
            dma((3,)), dma((steps,)), dma((steps + 2,)),
        ],
        name="residual",
    )(left_all, up_all, p_basis, q_terms)


def solution(mesh):
    in_specs = (P(("rep", "fsdp"), None), P(("rep", "fsdp"), None), P("fsdp", None, None))
    out_specs = (P("rep", "fsdp", None), P("fsdp", None, None), P("fsdp", None, None))
    return jax.shard_map(
        on_device, mesh=mesh, in_specs=in_specs, out_specs=out_specs, check_vma=False
    )
```

```python
import functools
import math

import jax
import jax.numpy as jnp
from jax import lax
from jax.experimental import pallas as pl
from jax.experimental.pallas import tpu as pltpu
from jax.sharding import PartitionSpec as P

MESH = pl.DeviceIdType.MESH
BF16 = jnp.bfloat16
F32 = jnp.float32


def two_terms(x):
    high = x.astype(BF16).astype(F32)
    return jnp.concatenate([high, x - high], axis=0).astype(BF16)


def folded(y):
    half = y.shape[0] // 2
    return y[:half] + y[half:]


def dot(a, b):
    return lax.dot_general(a, b, (((1,), (0,)), ((), ())), preferred_element_type=F32)


def dot_nt(a, b):
    return lax.dot_general(a, b, (((1,), (1,)), ((), ())), preferred_element_type=F32)


def exchange_kernel(
    cfg, act_hbm, up, q0, left_all, up_all, p_out, g_in,
    act, up_v, q_v, left, q_in, pc, rs_in, x_in, pfull, p_flat, cc, c_in, g_own,
    local_sem, q_s, q_r, u_s, u_r, b_s, b_r, rs_s, rs_r, x_s, x_r, ag_s, ag_r, c_s, c_r, g_s, g_r,
):
    reps, groups, chunks, part1, part2, parts = cfg
    me = lax.axis_index("rep")
    mf = lax.axis_index("fsdp")
    tok, width = act.shape
    rows = width // groups
    stride = reps // chunks
    piece = rows // parts
    rank = q_v.shape[0]
    cw = rows // chunks

    def ahead(d):
        return lax.rem(mf + d, groups)

    def remote(rep, group, src, dst, s, r):
        return pltpu.make_async_remote_copy(
            src_ref=src, dst_ref=dst, send_sem=s, recv_sem=r,
            device_id={"rep": rep, "fsdp": group}, device_id_type=MESH,
        )

    def loop(a, b, fn):
        def body(i, carry):
            fn(i)
            return carry

        lax.fori_loop(a, b, body, 0)

    load = pltpu.make_async_copy(act_hbm, act, local_sem.at[0])
    load_q = pltpu.make_async_copy(q0.at[0], q_v, local_sem.at[3])
    load_up = pltpu.make_async_copy(up, up_v, local_sem.at[4])
    load_q.start()
    load_up.start()
    load.start()
    barrier = pltpu.get_barrier_semaphore()
    def greet(rep, group):
        pl.semaphore_signal(barrier, inc=1, device_id={"rep": rep, "fsdp": group}, device_id_type=MESH)

    for d in range(1, groups):
        greet(me, ahead(d))
    loop(1, reps, lambda d: greet(lax.rem(me + d, reps), mf))
    my_tokens = pl.ds(pl.multiple_of(mf * tok, tok), tok)
    load_q.wait()
    load_up.wait()
    keep_up = pltpu.make_async_copy(up_v, up_all.at[my_tokens], local_sem.at[1])
    keep_up.start()
    upv = up_v[...]

    def columns(g):
        return pl.ds(pl.multiple_of(g * rows, rows), rows)

    def project(qv, g):
        w = folded(dot_nt(two_terms(qv), upv))
        val = folded(dot(two_terms(w), act[:, columns(g)]))
        for c in range(chunks):
            pc[c, g] = val[:, c * cw:(c + 1) * cw]

    def turn(i):
        at = pl.ds(pl.multiple_of(i * piece, piece), piece)
        left[at, :] = act[:, at].T

    load.wait()
    loop(0, (groups - 1) * parts, lambda i: turn(lax.rem(mf * parts + parts + i, groups * parts)))
    project(q_v[...], mf)
    keep_left = pltpu.make_async_copy(left.at[columns(mf)], left_all.at[:, my_tokens], local_sem.at[2])
    pl.semaphore_wait(barrier, reps + groups - 2)

    qs, us, bulk, cs = [], [], [], []
    for d in range(1, groups):
        qs.append(remote(me, ahead(d), q0.at[0], q_in.at[d - 1], q_s.at[d - 1], q_r.at[d - 1]))
        qs[-1].start()
    for d in range(1, groups):
        us.append(remote(me, ahead(d), up, up_all.at[my_tokens], u_s.at[d - 1], u_r.at[d - 1]))
        us[-1].start()

    mine = me // stride
    owner = lax.rem(me, stride) == 0

    def rs_copy(c):
        return remote(c * stride, mf, pc.at[c], rs_in.at[me], rs_s.at[c], rs_r.at[me])

    def rs_all(act_on):
        loop(1, chunks, lambda d: act_on(rs_copy(lax.rem(mine + d, chunks))))
        if stride > 1:
            @pl.when(jnp.logical_not(owner))
            def _():
                act_on(rs_copy(mine))

    loop(0, parts, lambda i: turn(mf * parts + i))
    keep_left.start()
    for d in range(1, groups):
        qs[groups - d - 1].wait_recv()
        project(q_in[groups - d - 1], ahead(d))
    rs_all(lambda c: c.start())

    for d in range(1, groups):
        bulk.append([
            remote(
                me, ahead(d),
                left.at[pl.ds(pl.multiple_of(ahead(d) * rows + k * piece, piece), piece)],
                left_all.at[pl.ds(k * piece, piece), my_tokens],
                b_s.at[d - 1, k], b_r.at[d - 1, k],
            )
            for k in range(parts)
        ])

    def send_bulk(a, b):
        for k in range(a, b):
            for row in bulk:
                row[k].start()

    send_bulk(0, part1)

    def ag_copy(i):
        j = lax.rem(me + i, reps)
        return remote(j, mf, pfull.at[mine], pfull.at[mine], ag_s.at[j], ag_r.at[mine])

    def ag_all(act_on):
        loop(1, reps, lambda i: act_on(ag_copy(i)))

    def across(d):
        return remote(me, ahead(d), x_in.at[mf], x_in.at[mf], x_s.at[d - 1], x_r.at[mf])

    def reduce_mine():
        rs_in[me] = pc[mine]

        def arrive(i):
            j = lax.rem(me + i, reps)
            remote(j, mf, rs_in.at[j], rs_in.at[j], rs_s.at[0], rs_r.at[j]).wait_recv()

        loop(1, reps, arrive)
        x_in[mf] = jnp.sum(rs_in[...], axis=0)
        for d in range(1, groups):
            across(d).start()
        for d in range(1, groups):
            g = ahead(d)
            remote(me, g, x_in.at[g], x_in.at[g], x_s.at[0], x_r.at[g]).wait_recv()
        pfull[mine] = jnp.sum(x_in[...], axis=0)
        ag_all(lambda c: c.start())

    def shares_done():
        ag_all(lambda c: c.wait_send())
        for d in range(1, groups):
            across(d).wait_send()

    def gather(i):
        c = lax.rem(mine + i, chunks)
        remote(c * stride, mf, pfull.at[c], pfull.at[c], ag_s.at[0], ag_r.at[c]).wait_recv()

    if stride > 1:
        pl.when(owner)(reduce_mine)
        pl.when(jnp.logical_not(owner))(lambda: gather(0))
    else:
        reduce_mine()
    send_bulk(part1, part2)
    loop(1, chunks, gather)

    v = pfull[...]
    row_at = lax.broadcasted_iota(jnp.int32, v.shape, 2)
    for i in range(rank):
        lead = v[:, :, i:i + 1, :]
        dots = jnp.sum(jnp.sum(v * lead, axis=0, keepdims=True), axis=3, keepdims=True)
        inv = lax.rsqrt(dots[:, :, i:i + 1, :] + 1e-06)
        unit = lead * inv
        v = jnp.where(row_at > i, v - (dots * inv) * unit, jnp.where(row_at == i, unit, v))
    for g in range(groups):
        for c in range(chunks):
            p_flat[g, :, c * cw:(c + 1) * cw] = v[c, g]
        t = folded(dot(two_terms(p_flat[g]), left[g * rows:(g + 1) * rows, :]))
        cc[g] = folded(dot(two_terms(t), upv))
    keep_p = pltpu.make_async_copy(p_flat.at[mf], p_out, local_sem.at[5])
    for d in range(1, groups):
        g = ahead(d)
        cs.append(remote(me, g, cc.at[g], c_in.at[d - 1], c_s.at[d - 1], c_r.at[d - 1]))
        cs[-1].start()
    send_bulk(part2, parts)
    keep_p.start()
    total = cc[mf]
    for c, got in zip(cs, range(groups - 1)):
        c.wait_recv()
        total = total + c_in[got]
    g_own[...] = total
    keep_g = pltpu.make_async_copy(g_own, g_in.at[me], local_sem.at[6])

    def g_copy(i):
        j = lax.rem(me + i, reps)
        return remote(j, mf, g_own, g_in.at[me], g_s.at[j], g_r.at[me])

    def g_arrive(i):
        j = lax.rem(me + i, reps)
        remote(j, mf, g_in.at[j], g_in.at[j], g_s.at[0], g_r.at[j]).wait_recv()

    loop(1, reps, lambda i: g_copy(i).start())
    keep_g.start()
    loop(1, reps, g_arrive)

    for c in qs + cs:
        c.wait_send()
    rs_all(lambda c: c.wait_send())
    if stride > 1:
        pl.when(owner)(shares_done)
    else:
        shares_done()
    loop(1, reps, lambda i: g_copy(i).wait_send())
    keep_up.wait()
    keep_left.wait()
    keep_p.wait()
    keep_g.wait()
    for c in us:
        c.wait()
    for k in range(parts):
        for row in bulk:
            row[k].wait()


def residual_kernel(
    reps, left_hbm, up_hbm, p_hbm, g_hbm, err, p_out, q_out, left, up, p, g, q, out, in_sem, left_sem, out_sem
):
    parts, step = left.shape[0], left.shape[1]
    small = [
        pltpu.make_async_copy(src, dst, in_sem.at[i])
        for i, (src, dst) in enumerate(((g_hbm, g), (p_hbm, p), (up_hbm, up)))
    ]
    loads = [
        pltpu.make_async_copy(left_hbm.at[pl.ds(k * step, step)], left.at[k], left_sem.at[k])
        for k in range(parts)
    ]
    for c in small + loads:
        c.start()
    for c in small:
        c.wait()
    q[...] = jnp.sum(g[...], axis=0)
    stores = [
        pltpu.make_async_copy(p, p_out.at[0], out_sem.at[parts]),
        pltpu.make_async_copy(q, q_out.at[0], out_sem.at[parts + 1]),
    ]
    for c in stores:
        c.start()
    upv = up[...]
    scaled = -(q[...] / reps)
    qh = scaled.astype(BF16).astype(F32)
    qst = jnp.concatenate([qh, qh, scaled - qh, scaled - qh], axis=0).astype(BF16)
    for k in range(parts):
        pv = p[:, k * step:(k + 1) * step]
        ph = pv.astype(BF16).astype(F32)
        pst = jnp.concatenate([ph, pv - ph, ph, pv - ph], axis=0).astype(BF16)
        low = lax.dot_general(pst, qst, (((0,), (0,)), ((), ())), preferred_element_type=F32)
        loads[k].wait()
        out[k] = (dot(left[k], upv) + low).astype(BF16)
        c = pltpu.make_async_copy(out.at[k], err.at[0, pl.ds(k * step, step)], out_sem.at[k])
        c.start()
        stores.append(c)
    for c in stores:
        c.wait()


def on_device(activations, upstream, q_start):
    reps = lax.axis_size("rep")
    groups = lax.axis_size("fsdp")
    tok, width = activations.shape
    kvw = upstream.shape[1]
    rank = q_start.shape[1]
    rows = width // groups
    chunks = math.gcd(reps, rows // 128)
    cw = rows // chunks
    parts = 16
    cfg = (reps, groups, chunks, 6, 11, parts)
    hbm = pl.BlockSpec(memory_space=pl.ANY)
    dma = pltpu.SemaphoreType.DMA
    peers = groups - 1
    left_all, up_all, p_basis, q_terms = pl.pallas_call(
        functools.partial(exchange_kernel, cfg),
        out_shape=(
            jax.ShapeDtypeStruct((rows, groups * tok), BF16),
            jax.ShapeDtypeStruct((groups * tok, kvw), BF16),
            jax.ShapeDtypeStruct((rank, rows), F32),
            jax.ShapeDtypeStruct((reps, rank, kvw), F32),
        ),
        in_specs=[hbm] * 3,
        out_specs=(hbm,) * 4,
        scratch_shapes=[
            pltpu.VMEM((tok, width), BF16),
            pltpu.VMEM((tok, kvw), BF16),
            pltpu.VMEM((rank, kvw), F32),
            pltpu.VMEM((width, tok), BF16),
            pltpu.VMEM((peers, rank, kvw), F32),
            pltpu.VMEM((chunks, groups, rank, cw), F32),
            pltpu.VMEM((reps, groups, rank, cw), F32),
            pltpu.VMEM((groups, groups, rank, cw), F32),
            pltpu.VMEM((chunks, groups, rank, cw), F32),
            pltpu.VMEM((groups, rank, rows), F32),
            pltpu.VMEM((groups, rank, kvw), F32),
            pltpu.VMEM((peers, rank, kvw), F32),
            pltpu.VMEM((rank, kvw), F32),
            dma((7,)),
            dma((peers,)), dma((peers,)),
            dma((peers,)), dma((peers,)),
            dma((peers, parts)), dma((peers, parts)),
            dma((chunks,)), dma((reps,)),
            dma((peers,)), dma((groups,)),
            dma((reps,)), dma((chunks,)),
            dma((peers,)), dma((peers,)),
            dma((reps,)), dma((reps,)),
        ],
        compiler_params=pltpu.CompilerParams(collective_id=0, has_side_effects=True),
        name="exchange",
    )(activations, upstream, q_start)
    steps = 8
    step = rows // steps
    return pl.pallas_call(
        functools.partial(residual_kernel, reps),
        out_shape=(
            jax.ShapeDtypeStruct((1, rows, kvw), BF16),
            jax.ShapeDtypeStruct((1, rank, rows), F32),
            jax.ShapeDtypeStruct((1, rank, kvw), F32),
        ),
        in_specs=[hbm] * 4,
        out_specs=(hbm,) * 3,
        scratch_shapes=[
            pltpu.VMEM((steps, step, groups * tok), BF16),
            pltpu.VMEM((groups * tok, kvw), BF16),
            pltpu.VMEM((rank, rows), F32),
            pltpu.VMEM((reps, rank, kvw), F32),
            pltpu.VMEM((rank, kvw), F32),
            pltpu.VMEM((steps, step, kvw), BF16),
            dma((3,)), dma((steps,)), dma((steps + 2,)),
        ],
        name="residual",
    )(left_all, up_all, p_basis, q_terms)


def solution(mesh):
    in_specs = (P(("rep", "fsdp"), None), P(("rep", "fsdp"), None), P("fsdp", None, None))
    out_specs = (P("rep", "fsdp", None), P("fsdp", None, None), P("fsdp", None, None))
    return jax.shard_map(
        on_device, mesh=mesh, in_specs=in_specs, out_specs=out_specs, check_vma=False
    )
```
